32 devices in a mesh: ctx: 8 (over z, y), tp: 4 (over x, core).
Axes of the slice: x: 2, y: 2, z: 4, core: 2. Of those that a mesh axis runs over, the one named last changes fastest.
Arguments:
- tokens: bfloat16 [1024, 8192], P('ctx', 'tp'), may hold values from -6 to 6
- query_mr: bfloat16 [1024, 8192], P('ctx', 'tp'), may hold values from -6 to 6
- key_mr: bfloat16 [1024, 8192], P('ctx', 'tp'), may hold values from -6 to 6
- gain_mr: float32 [8192], P('tp'), may hold values from 0.5 to 1.5
- filter_mr: bfloat16 [512, 128], P('tp'), may hold values from -0.5 to 0.5
- query_li: bfloat16 [1024, 8192], P('ctx', 'tp'), may hold values from -6 to 6
- key_li: bfloat16 [1024, 8192], P('ctx', 'tp'), may hold values from -6 to 6
- gain_li: float32 [8192], P('tp'), may hold values from 0.5 to 1.5
- log_rates: float32 [16, 8192], P(None, 'tp'), may hold values from -12 to -3, as said below
- retain: float32 [1024], P('ctx'), may hold values from 0.6 to 1, as said below
- residues: float32 [16, 8192], P(None, 'tp'), may hold values from -1.5 to 1.5
- cotangent: bfloat16 [1024, 8192], P('ctx', 'tp'), may hold values from -6 to 6
Outputs:
- mixed: bfloat16 [1024, 8192], P('ctx', 'tp')
- grad_tokens: bfloat16 [1024, 8192], P('ctx', 'tp')
- grad_query_mr: bfloat16 [1024, 8192], P('ctx', 'tp')
- gradient_key_medium: bfloat16 [1024, 8192], P('ctx', 'tp')
- grad_query_li: bfloat16 [1024, 8192], P('ctx', 'tp')
- grad_key_li: bfloat16 [1024, 8192], P('ctx', 'tp')
- grad_gain_mr: float32 [8192], P('tp')
- grad_gain_li: float32 [8192], P('tp')
- grad_filter_mr: float32 [512, 128], P('tp')
- grad_residues: float32 [16, 8192], P(None, 'tp')
- grad_log_rates: float32 [16, 8192], P(None, 'tp')
The draws below stay inside these ranges and needn't reach their ends.
Inputs may be any that keep to these rules, and one draw needn't show every extreme that they name: `log_rates`: each entry is the logarithm of a decay rate per position. `retain`: a share of state kept at a position, 1 at most positions.
All inputs are finite; a program needn't handle non-finite values.
Results may differ from the reference program's by a relative error of at most 0.0054.
Values may be sent and summed in bfloat16 or wider, within the bound.
A program may use at most 128 MiB of HBM per device.

```python
import jax
import jax.numpy as jnp
from jax import lax

D = 8192
FILT = 128
MODES = 16
GROUP = 16
TOK_DEV = 128
WINDOW_SITES = 1024


def draw_log_rates(key, part):
    select_key, slow_key, fast_key = jax.random.split(key, 3)
    share = 0.5
    slow = jax.random.uniform(select_key, (MODES, D)) < share
    slow_log = jax.random.uniform(slow_key, (MODES, D), minval=jnp.log(0.25 / WINDOW_SITES), maxval=jnp.log(1.0 / WINDOW_SITES))
    fast_log = jax.random.uniform(fast_key, (MODES, D), minval=jnp.log(1.0 / 50.0), maxval=jnp.log(1.0 / 30.0))
    return jnp.where(slow, slow_log, fast_log).astype(jnp.float32)


def draw_retain(key, part):
    locus_random_seed, value_key = jax.random.split(key, 2)
    tile_extent = jax.random.uniform(locus_random_seed, (WINDOW_SITES,)) < 4.0 / WINDOW_SITES
    doubling_tier = jax.random.uniform(value_key, (WINDOW_SITES,), minval=0.6, maxval=0.85)
    return jnp.where(tile_extent, doubling_tier, 1.0).astype(jnp.float32)


def block_scale(own_key, extent, cuts, low, largest):
    level = 1.0
    for axis_at, shards_of in cuts:
        draws = jax.random.uniform(jax.random.fold_in(jax.random.fold_in(own_key, 6), axis_at), (shards_of,), jnp.float32, low / len(cuts), largest / len(cuts))
        level = level * jnp.repeat(jnp.exp(draws), extent[axis_at] // shards_of).reshape((-1,) + (1,) * (len(extent) - 1 - axis_at))
    return level


def bell_draw(key, shape, spread, reach, cuts=(), kind=jnp.bfloat16):
    values = jax.random.normal(key, shape, jnp.float32) * spread
    if len(cuts) > 0:
        values = block_scale(key, shape, cuts, -0.22, 0.18) * values
    return jnp.clip(values, min=-reach, max=reach).astype(kind)


def setup_inputs(seed: int = 0) -> dict:
    seeds = jax.random.split(jax.random.key(seed), 13)
    tokens = bell_draw(seeds[0], (WINDOW_SITES, D), 1.0, 6.0, ((0, 8), (1, 4)))
    query_mr = bell_draw(seeds[1], (WINDOW_SITES, D), 1.0, 6.0, ((0, 8), (1, 4)))
    key_mr = bell_draw(seeds[2], (WINDOW_SITES, D), 1.0, 6.0, ((0, 8), (1, 4)))
    gain_mr = jnp.clip(1.0 + 0.1 * jax.random.normal(seeds[3], (D,), jnp.float32), 0.5, 1.5)
    filter_mr = bell_draw(seeds[4], (D // GROUP, FILT), FILT ** -0.5, 0.5, ((0, 4),))
    query_li = bell_draw(seeds[5], (WINDOW_SITES, D), 1.0, 6.0, ((0, 8), (1, 4)))
    key_li = bell_draw(seeds[6], (WINDOW_SITES, D), 1.0, 6.0, ((0, 8), (1, 4)))
    gain_li = jnp.clip(1.0 + 0.1 * jax.random.normal(seeds[7], (D,), jnp.float32), 0.5, 1.5)
    log_rates = draw_log_rates(jax.random.fold_in(seeds[12], 71), 0)
    retain = draw_retain(jax.random.fold_in(seeds[12], 71), 0)
    residues = bell_draw(seeds[10], (MODES, D), 0.25, 1.5, ((1, 4),), jnp.float32)
    cotangent = bell_draw(seeds[11], (WINDOW_SITES, D), 1.0, 6.0, ((0, 8), (1, 4)))
    return dict(tokens=tokens, query_mr=query_mr, key_mr=key_mr, gain_mr=gain_mr, filter_mr=filter_mr, query_li=query_li, key_li=key_li, gain_li=gain_li, log_rates=log_rates, retain=retain, residues=residues, cotangent=cotangent)


EPSILON = 1e-06

def rounded(value):
    narrow = lax.optimization_barrier(value.astype(jnp.bfloat16))
    return value + lax.stop_gradient(narrow.astype(jnp.float32) - value)

def rms_norm(values, gain):
    power = lax.optimization_barrier(jnp.mean(values * values, axis=1, keepdims=True))
    return values * gain[None, :] * lax.rsqrt(power + EPSILON)

def causal_groups(values, filters):
    groups, width = filters.shape
    row_ids = lax.broadcasted_iota(jnp.int32, (width, width), 0)
    column_indices = lax.broadcasted_iota(jnp.int32, (width, width), 1)
    lag_index = (row_ids - column_indices) % width
    table = jnp.take(filters, lag_index, axis=1)
    beneath_diagonal_strip = jnp.where(row_ids >= column_indices, table, jnp.zeros_like(table))
    upper_band = jnp.where(row_ids < column_indices, table, jnp.zeros_like(table))
    total, channels = values.shape
    padded = jnp.concatenate([jnp.zeros((width, channels), values.dtype), values], axis=0)
    blocks = padded.reshape(total // width + 1, width, groups, channels // groups)
    result = jnp.einsum('gij,bjgc->bigc', beneath_diagonal_strip, blocks[1:], precision=lax.Precision.HIGHEST)
    result = result + jnp.einsum('gij,bjgc->bigc', upper_band, blocks[:-1], precision=lax.Precision.HIGHEST)
    return result.reshape(total, channels)

def modal_filter(values, log_rates, retain, residues):
    rates = jnp.exp(log_rates)
    poles = jnp.exp(-rates)
    weight = residues * jnp.sqrt(-jnp.expm1(-2.0 * rates))
    total, channels = values.shape
    value_blocks = values.reshape(total // TOK_DEV, TOK_DEV, channels)
    retain_blocks = retain.reshape(total // TOK_DEV, TOK_DEV)

    def inner(carry, block):
        block_values, block_retain = block

        def advance(state, item):
            value_row, keep = item
            state = poles * keep * state + value_row[None, :]
            return (state, lax.optimization_barrier(jnp.sum(weight * state, axis=0)))
        return lax.scan(advance, carry, (block_values, block_retain))
    start = jnp.zeros(log_rates.shape, jnp.float32)
    final, outputs = lax.scan(jax.checkpoint(inner), start, (value_blocks, retain_blocks))
    return outputs.reshape(total, channels)

def forward(tokens, query_mr, key_mr, gain_mr, filter_mr, query_li, key_li, gain_li, log_rates, retain, residues):
    normed_in = rms_norm(tokens, gain_mr)
    mixed_in = rounded(key_mr * normed_in)
    conv_mr = causal_groups(mixed_in, filter_mr)
    middle = rounded(tokens + query_mr * conv_mr)
    normed_mid = rms_norm(middle, gain_li)
    conv_li = modal_filter(key_li * normed_mid, log_rates, retain, residues)
    return middle + query_li * conv_li

def reference(tokens, query_mr, key_mr, gain_mr, filter_mr, query_li, key_li, gain_li, log_rates, retain, residues, cotangent):
    inputs = (tokens, query_mr, key_mr, gain_mr, filter_mr, query_li, key_li, gain_li, log_rates, retain, residues)
    floats = tuple((item.astype(jnp.float32) for item in inputs))
    output, pullback = jax.vjp(forward, *floats)
    grads = pullback(cotangent.astype(jnp.float32))
    factor = lax.rsqrt(jnp.asarray(WINDOW_SITES, jnp.float32))
    return (output.astype(jnp.bfloat16), grads[0].astype(jnp.bfloat16), grads[1].astype(jnp.bfloat16), grads[2].astype(jnp.bfloat16), grads[5].astype(jnp.bfloat16), grads[6].astype(jnp.bfloat16), grads[3] * factor, grads[7] * factor, grads[4] * factor, grads[10] * factor, grads[8] * factor)
```

```python
import functools
import math

import jax
import jax.numpy as jnp
from jax import lax
from jax.experimental import pallas as pl
from jax.experimental.pallas import tpu as pltpu
from jax.sharding import PartitionSpec as P

EPSILON = 1e-06
LANES = 128
F32 = jnp.float32
BF16 = jnp.bfloat16
MESH = pl.DeviceIdType.MESH


def vmem(count):
    return [pl.BlockSpec(memory_space=pltpu.VMEM)] * count


def local_call(kernel, name, outs, args, scratch=(), flops=10_000_000):
    return pl.pallas_call(
        kernel,
        name=name,
        out_shape=[jax.ShapeDtypeStruct(s, d) for s, d in outs],
        in_specs=vmem(len(args)),
        out_specs=vmem(len(outs)),
        scratch_shapes=list(scratch),
        cost_estimate=pl.CostEstimate(flops=flops, bytes_accessed=8_000_000, transcendentals=0),
    )(*args)


def exchange(items, sizes, cid, name):
    count = len(items)
    axes = []
    for _, axis, _ in items:
        if axis not in axes:
            axes.append(axis)
    remote = sum(sizes[axis] - 1 for _, axis, _ in items)

    def kernel(*refs):
        ins, outs = refs[:count], refs[count : 2 * count]
        send, recv, own = refs[2 * count :]
        barrier = pltpu.get_barrier_semaphore()
        greeted = 0
        for axis in axes:
            me = lax.axis_index(axis)
            for step in range(1, sizes[axis]):
                peer = lax.rem(me + step, sizes[axis])
                pl.semaphore_signal(barrier, inc=1, device_id={axis: peer}, device_id_type=MESH)
                greeted += 1
        pl.semaphore_wait(barrier, greeted)
        copies = []
        slot = 0
        for number, (_, axis, scatter) in enumerate(items):
            me = lax.axis_index(axis)
            for step in range(1, sizes[axis]):
                peer = lax.rem(me + step, sizes[axis])
                source = ins[number].at[peer] if scatter else ins[number]
                copy = pltpu.make_async_remote_copy(
                    src_ref=source,
                    dst_ref=outs[number].at[me],
                    send_sem=send.at[slot],
                    recv_sem=recv.at[slot],
                    device_id={axis: peer},
                    device_id_type=MESH,
                )
                copy.start()
                copies.append(copy)
                slot += 1
            source = ins[number].at[me] if scatter else ins[number]
            copy = pltpu.make_async_copy(source, outs[number].at[me], own.at[number])
            copy.start()
            copies.append(copy)
        for copy in copies:
            copy.wait()

    outs = []
    for array, axis, scatter in items:
        shape = array.shape if scatter else (sizes[axis],) + array.shape
        outs.append(jax.ShapeDtypeStruct(shape, array.dtype))
    return pl.pallas_call(
        kernel,
        name=name,
        out_shape=outs,
        in_specs=vmem(count),
        out_specs=vmem(count),
        scratch_shapes=[
            pltpu.SemaphoreType.DMA((remote,)),
            pltpu.SemaphoreType.DMA((remote,)),
            pltpu.SemaphoreType.DMA((count,)),
        ],
        compiler_params=pltpu.CompilerParams(collective_id=cid, has_side_effects=True),
    )(*[array for array, _, _ in items])


def column(row):
    return jnp.broadcast_to(row, (LANES, LANES)).T


def row8(partial):
    total = jnp.sum(partial, axis=1, keepdims=True)
    return jnp.broadcast_to(total, partial.shape).T[:8]


def lane_tile(j):
    return pl.ds(pl.multiple_of(j * LANES, LANES), LANES)


def total_row(ref):
    out = ref[0]
    for k in range(1, ref.shape[0]):
        out = out + ref[k]
    return out[:1]


def begin_kernel(modes, x_ref, cot_ref, q_ref, keep_ref, p_ref, w_ref, pow_ref, r_ref, g_ref, lead_ref):
    rows, channels = x_ref.shape
    tiles = channels // LANES
    lanes = lax.broadcasted_iota(jnp.int32, (8, LANES), 1)
    run = keep_ref[...]
    step = 1
    while step < LANES:
        run = run * jnp.where(lanes >= step, pltpu.roll(run, step, 1), 1.0)
        step *= 2
    r_ref[...] = run
    r_col = column(run[:1])
    total = jnp.zeros((rows, LANES), F32)
    for j in range(tiles):
        at = slice(j * LANES, (j + 1) * LANES)
        x = x_ref[:, at].astype(F32)
        total = total + x * x
        g_ref[pl.ds(j, rows, stride=tiles), :] = (
            cot_ref[:, at].astype(F32) * q_ref[:, at].astype(F32) * r_col
        )
    pow_ref[...] = row8(total)
    sub = min(8, tiles)
    for b in range(tiles // sub):
        where = [pl.ds(n * tiles + b * sub, sub) for n in range(modes)]
        pole = [p_ref[at, :] for at in where]

        def back(i, units, b=b, pole=pole):
            t = rows - 1 - i
            g = g_ref[pl.ds(pl.multiple_of(t * tiles + b * sub, sub), sub), :]
            return tuple(pole[n] * units[n] + g for n in range(modes))

        units = lax.fori_loop(
            0, rows, back, tuple(jnp.zeros((sub, LANES), F32) for _ in range(modes)), unroll=4
        )
        for n in range(modes):
            lead_ref[where[n], :] = (w_ref[where[n], :] * pole[n] * units[n]).astype(BF16)


def carried(part_ref, r_all_ref, pass_ref, ahead, reverse):
    count = part_ref.shape[0]
    order = range(count - 1, 0, -1) if reverse else range(count - 1)
    acc = jnp.zeros(pass_ref.shape, F32)
    for m in order:
        share = jnp.broadcast_to(r_all_ref[m][:1, LANES - 1 :], (1, LANES))
        new = part_ref[m].astype(F32) + pass_ref[...] * share * acc
        live = m > ahead if reverse else m < ahead
        acc = jnp.where(live, new, acc)
    return acc


def adjoint_kernel(
    modes, g_ref, p_ref, w_ref, pass_ref, lead_ref, r_all_ref, r_ref, v_ref, q_out_ref, v3_ref
):
    rows, channels = v_ref.shape
    tiles = channels // LANES
    r_row = r_ref[:1, :]
    r_end = jnp.broadcast_to(r_row[:, LANES - 1 :], (1, LANES))
    q_out_ref[...] = carried(lead_ref, r_all_ref, pass_ref, lax.axis_index("ctx"), True) * r_end
    sub = min(8, tiles)
    for b in range(tiles // sub):
        where = [pl.ds(n * tiles + b * sub, sub) for n in range(modes)]
        pole = [p_ref[at, :] for at in where]
        weight = [w_ref[at, :] for at in where]
        last = pl.ds((rows - 1) * tiles + b * sub, sub)
        g = g_ref[last, :]
        start = [q_out_ref[where[n], :] + weight[n] * g for n in range(modes)]
        v3_ref[last, :] = functools.reduce(lambda a, c: a + c, start)

        def back(i, adj, b=b, pole=pole, weight=weight):
            at = pl.ds(pl.multiple_of((rows - 2 - i) * tiles + b * sub, sub), sub)
            g = g_ref[at, :]
            adj = tuple(pole[n] * adj[n] + weight[n] * g for n in range(modes))
            sums = list(adj)
            while len(sums) > 1:
                sums = [sums[k] + sums[k + 1] for k in range(0, len(sums), 2)]
            v3_ref[at, :] = sums[0]
            return adj

        lax.fori_loop(0, rows - 1, back, tuple(start), unroll=2)
    inverse = 1.0 / column(r_row)
    for j in range(tiles):
        v_ref[:, j * LANES : (j + 1) * LANES] = v3_ref[pl.ds(j, rows, stride=tiles), :] * inverse


def mix_kernel(width, x_ref, key_ref, gain_ref, pow_ref, mixed_ref):
    scale = column(lax.rsqrt(total_row(pow_ref) / width + EPSILON))
    for j in range(x_ref.shape[1] // LANES):
        at = slice(j * LANES, (j + 1) * LANES)
        normed = x_ref[:, at].astype(F32) * gain_ref[:, at] * scale
        mixed_ref[:, at] = (key_ref[:, at].astype(F32) * normed).astype(BF16)


def conv_kernel(
    members, x_ref, q_ref, mixed_ref, prev_ref, flip_ref, v_ref, key_ref, gain_ref,
    conv_ref, mid_ref, sums_ref,
):
    rows, channels = x_ref.shape
    fold = LANES // members
    row_ids = lax.broadcasted_iota(jnp.int32, (rows, LANES), 0)
    col_ids = lax.broadcasted_iota(jnp.int32, (rows, LANES), 1)
    owner = col_ids // members
    fresh = lax.axis_index("ctx") > 0

    def tile(j, sums):
        at = lane_tile(j)
        prev = prev_ref[:, at]
        prev = jnp.where(fresh, prev, jnp.zeros_like(prev))
        both = jnp.concatenate([prev, mixed_ref[:, at]], axis=0)
        taps = flip_ref[pl.ds(pl.multiple_of(j * fold, fold), fold), :]
        conv = jnp.zeros((rows, LANES), F32)
        for g in range(fold):
            table = pltpu.roll(
                jnp.broadcast_to(taps[g : g + 1], (rows, LANES)), 0, 1, stride=1, stride_axis=0
            )
            low = jnp.where(row_ids >= col_ids, table, 0.0).astype(BF16)
            high = jnp.where(row_ids < col_ids, table, 0.0).astype(BF16)
            out = jnp.dot(
                jnp.concatenate([high, low], axis=1), both, preferred_element_type=F32
            )
            conv = jnp.where(owner == g, out, conv)
        conv_ref[:, at] = conv
        mid = (x_ref[:, at].astype(F32) + q_ref[:, at].astype(F32) * conv).astype(BF16)
        mid_ref[:, at] = mid
        mid = mid.astype(F32)
        inner = v_ref[:, at] * key_ref[:, at].astype(F32) * gain_ref[:, at] * mid
        return (sums[0] + mid * mid, sums[1] + inner)

    zero = jnp.zeros((rows, LANES), F32)
    power, inner = lax.fori_loop(0, channels // LANES, tile, (zero, zero))
    sums_ref[0] = row8(power)
    sums_ref[1] = row8(inner)


def middle_kernel(
    width, mid_ref, key_ref, gain_ref, v_ref, cot_ref, qmr_ref, conv_ref, r_ref, sums_ref,
    gkey_ref, gmid_ref, gq_ref, gconv_ref, gain_part_ref, u_ref,
):
    rows, channels = v_ref.shape
    tiles = channels // LANES
    sums = sums_ref[0]
    for k in range(1, sums_ref.shape[0]):
        sums = sums + sums_ref[k]
    scale = column(lax.rsqrt(sums[0][:1] / width + EPSILON))
    pull = scale * scale * scale * column(sums[1][:1]) / width
    inverse = 1.0 / column(r_ref[:1, :])
    for j in range(tiles):
        at = slice(j * LANES, (j + 1) * LANES)
        mid = mid_ref[:, at].astype(F32)
        key = key_ref[:, at].astype(F32)
        gain = gain_ref[:, at]
        v = v_ref[:, at]
        normed = mid * gain * scale
        gkey_ref[:, at] = (v * normed).astype(BF16)
        u_ref[pl.ds(j, rows, stride=tiles), :] = key * normed * inverse
        grad = v * key
        gain_part_ref[:, at] = jnp.sum(grad * mid * scale, axis=0, keepdims=True)
        gmid = cot_ref[:, at].astype(F32) + gain * scale * grad - mid * pull
        gmid_ref[:, at] = gmid
        gq_ref[:, at] = (gmid * conv_ref[:, at]).astype(BF16)
        gconv_ref[:, at] = (gmid * qmr_ref[:, at].astype(F32)).astype(BF16)


def finish_kernel(modes, u_ref, p_ref, r_ref, out_ref):
    tiles = p_ref.shape[0] // modes
    rows = u_ref.shape[0] // tiles
    r_end = jnp.broadcast_to(r_ref[:1, LANES - 1 :], (1, LANES))
    sub = min(8, tiles)
    for b in range(tiles // sub):
        where = [pl.ds(n * tiles + b * sub, sub) for n in range(modes)]
        pole = [p_ref[at, :] for at in where]

        def step(t, states, b=b, pole=pole):
            u = u_ref[pl.ds(pl.multiple_of(t * tiles + b * sub, sub), sub), :]
            return tuple(pole[n] * states[n] + u for n in range(modes))

        states = lax.fori_loop(
            0, rows, step, tuple(jnp.zeros((sub, LANES), F32) for _ in range(modes)), unroll=4
        )
        for n in range(modes):
            out_ref[where[n], :] = (states[n] * r_end).astype(BF16)


def state_kernel(
    modes, u_ref, g_ref, p_ref, w_ref, pass_ref, fin_ref, r_all_ref, r_ref, q_ref, c_ref,
    mid_ref, cot_ref, qli_ref, mixed_ref, gq_ref, res_ref, rate_ref, y_ref, in_ref,
):
    rows, channels = mid_ref.shape
    tiles = channels // LANES
    in_ref[...] = carried(fin_ref, r_all_ref, pass_ref, lax.axis_index("ctx"), False)
    sub = min(8, tiles)
    half = min(8, modes)
    zero = jnp.zeros((sub, LANES), F32)
    for b in range(tiles // sub):
        for first in range(0, modes, half):
            where = [pl.ds((first + n) * tiles + b * sub, sub) for n in range(half)]
            pole = [p_ref[at, :] for at in where]
            weight = [w_ref[at, :] for at in where]

            def step(t, carry, b=b, first=first, pole=pole, weight=weight):
                at = pl.ds(pl.multiple_of(t * tiles + b * sub, sub), sub)
                u = u_ref[at, :]
                g = g_ref[at, :]
                states, slopes, wsum, psum = carry
                slopes = tuple(pole[n] * slopes[n] + states[n] for n in range(half))
                states = tuple(pole[n] * states[n] + u for n in range(half))
                wsum = tuple(wsum[n] + g * states[n] for n in range(half))
                psum = tuple(psum[n] + g * slopes[n] for n in range(half))
                sums = [weight[n] * states[n] for n in range(half)]
                while len(sums) > 1:
                    sums = [sums[k] + sums[k + 1] for k in range(0, len(sums), 2)]
                if first == 0:
                    y_ref[at, :] = sums[0]
                else:
                    y_ref[at, :] = y_ref[at, :] + sums[0]
                return (states, slopes, wsum, psum)

            begin = tuple(in_ref[at, :] for at in where)
            zeros = (zero,) * half
            _, slopes, wsum, psum = lax.fori_loop(
                0, rows, step, (begin, zeros, zeros, zeros), unroll=2
            )
            for n in range(half):
                at = where[n]
                pgrad = weight[n] * psum[n] + q_ref[at, :] * slopes[n]
                res_ref[at, :] = c_ref[0, at, :] * wsum[n]
                rate_ref[at, :] = c_ref[1, at, :] * wsum[n] - c_ref[2, at, :] * pgrad
    r_col = column(r_ref[:1, :])
    for j in range(tiles):
        at = slice(j * LANES, (j + 1) * LANES)
        conv = y_ref[pl.ds(j, rows, stride=tiles), :] * r_col
        mixed_ref[:, at] = (
            mid_ref[:, at].astype(F32) + qli_ref[:, at].astype(F32) * conv
        ).astype(BF16)
        gq_ref[:, at] = (cot_ref[:, at].astype(F32) * conv).astype(BF16)


def back_kernel(
    members, width, gconv_ref, next_ref, mixed_ref, prev_ref, filt_ref, x_ref, key_ref, gain_ref,
    pow_ref, gkey_ref, gnorm_ref, gain_part_ref, inner_ref, fgrad_ref,
):
    rows, channels = x_ref.shape
    fold = LANES // members
    row_ids = lax.broadcasted_iota(jnp.int32, (rows, LANES), 0)
    col_ids = lax.broadcasted_iota(jnp.int32, (rows, LANES), 1)
    owner = col_ids // members
    flip = jnp.where(row_ids + col_ids == rows - 1, 1.0, 0.0).astype(BF16)
    place = lax.axis_index("ctx")
    fresh = place > 0
    more = place < lax.axis_size("ctx") - 1
    scale = column(lax.rsqrt(total_row(pow_ref) / width + EPSILON))

    def tile(j, inner):
        at = lane_tile(j)
        prev = prev_ref[:, at]
        prev = jnp.where(fresh, prev, jnp.zeros_like(prev))
        later = next_ref[:, at]
        later = jnp.where(more, later, jnp.zeros_like(later))
        own = gconv_ref[:, at]
        both = jnp.concatenate([own, later], axis=0)
        turned = jnp.concatenate(
            [
                jnp.dot(flip, mixed_ref[:, at], preferred_element_type=F32).astype(BF16),
                jnp.dot(flip, prev, preferred_element_type=F32).astype(BF16),
            ],
            axis=0,
        )
        rows_at = pl.ds(pl.multiple_of(j * fold, fold), fold)
        taps = filt_ref[rows_at, :]
        gmix = jnp.zeros((rows, LANES), F32)
        grads = []
        for g in range(fold):
            table = pltpu.roll(
                jnp.broadcast_to(taps[g : g + 1], (rows, LANES)), 0, 1, stride=1, stride_axis=0
            )
            low = jnp.where(col_ids >= row_ids, table, 0.0).astype(BF16)
            high = jnp.where(col_ids < row_ids, table, 0.0).astype(BF16)
            out = jnp.dot(jnp.concatenate([low, high], axis=1), both, preferred_element_type=F32)
            gmix = jnp.where(owner == g, out, gmix)
            mine = jnp.where(owner == g, own, jnp.zeros_like(own))
            pair = lax.dot_general(
                turned, mine, (((1,), (1,)), ((), ())), preferred_element_type=F32
            )
            pair = jnp.where(col_ids >= rows - 1 - row_ids, pair[:rows], pair[rows:])
            pair = pltpu.roll(pair, 1, 1, stride=1, stride_axis=0)
            grads.append(jnp.sum(pair, axis=0, keepdims=True))
        fgrad_ref[rows_at, :] = jnp.concatenate(grads, axis=0)
        x = x_ref[:, at].astype(F32)
        gain = gain_ref[:, at]
        gkey_ref[:, at] = (gmix * (x * gain * scale)).astype(BF16)
        gnorm = gmix * key_ref[:, at].astype(F32)
        gnorm_ref[:, at] = gnorm
        gain_part_ref[:, at] = jnp.sum(gnorm * x * scale, axis=0, keepdims=True)
        return inner + gnorm * gain * x

    inner = lax.fori_loop(0, channels // LANES, tile, jnp.zeros((rows, LANES), F32))
    inner_ref[...] = row8(inner)


def last_kernel(
    width, factor, x_ref, gain_ref, gmid_ref, gnorm_ref, pow_ref, inner_ref, parts_ref,
    out_ref, sum_ref,
):
    scale = column(lax.rsqrt(total_row(pow_ref) / width + EPSILON))
    pull = scale * scale * scale * column(total_row(inner_ref)) / width
    for j in range(x_ref.shape[1] // LANES):
        at = slice(j * LANES, (j + 1) * LANES)
        out_ref[:, at] = (
            gmid_ref[:, at]
            + gain_ref[:, at] * scale * gnorm_ref[:, at]
            - x_ref[:, at].astype(F32) * pull
        ).astype(BF16)
    total = parts_ref[0].astype(F32)
    for k in range(1, parts_ref.shape[0]):
        total = total + parts_ref[k].astype(F32)
    sum_ref[...] = (total * factor).astype(BF16)


def body(
    sizes,
    tokens,
    query_mr,
    key_mr,
    gain_mr,
    filter_mr,
    query_li,
    key_li,
    gain_li,
    log_rates,
    retain,
    residues,
    cotangent,
):
    rows, channels = tokens.shape
    groups, taps = filter_mr.shape
    members = channels // groups
    modes = log_rates.shape[0]
    tiles = channels // LANES
    ctx, tp = sizes["ctx"], sizes["tp"]
    width = channels * tp
    factor = 1.0 / math.sqrt(rows * ctx)
    flat = (modes * tiles, LANES)
    full = (rows, channels)

    rates = jnp.exp(log_rates.reshape(flat))
    resid = residues.reshape(flat)
    poles = jnp.exp(-rates)
    spread = jnp.sqrt(-jnp.expm1(-2.0 * rates))
    weight = resid * spread
    passing = jnp.exp(-rows * rates)
    consts = jnp.stack([spread, rates * resid * jnp.exp(-2.0 * rates) / spread, rates * poles])
    keep = jnp.broadcast_to(retain[None, :], (8, rows))
    wide = filter_mr.astype(F32)
    flipped = jnp.concatenate([wide[:, :1], wide[:, :0:-1]], axis=1)
    gain_mr = gain_mr[None, :]
    gain_li = gain_li[None, :]

    power, shares, g_seq, lead = local_call(
        functools.partial(begin_kernel, modes),
        "begin",
        [((8, rows), F32), ((8, rows), F32), ((rows * tiles, LANES), F32), (flat, BF16)],
        (tokens, cotangent, query_li, keep, poles, weight),
    )
    power_all, = exchange([(power, "tp", False)], sizes, 1, "gather_power")
    mixed_in, = local_call(
        functools.partial(mix_kernel, width), "mix", [(full, BF16)],
        (tokens, key_mr, gain_mr, power_all),
    )
    before = lax.ppermute(mixed_in, "ctx", [(k, k + 1) for k in range(ctx - 1)])
    lead_all, shares_all = exchange(
        [(lead, "ctx", False), (shares, "ctx", False)], sizes, 2, "gather_lead"
    )
    v, pulled = local_call(
        functools.partial(adjoint_kernel, modes),
        "adjoint",
        [(full, F32), (flat, F32)],
        (g_seq, poles, weight, passing, lead_all, shares_all, shares),
        [pltpu.VMEM((rows * tiles, LANES), F32)],
    )
    conv, middle, sums = local_call(
        functools.partial(conv_kernel, members),
        "conv",
        [(full, F32), (full, BF16), ((2, 8, rows), F32)],
        (tokens, query_mr, mixed_in, before, flipped, v, key_li, gain_li),
    )
    sums_all, = exchange([(sums, "tp", False)], sizes, 3, "gather_middle")
    grad_key_li, grad_mid, grad_query_mr, grad_conv, gain_li_part, u_seq = local_call(
        functools.partial(middle_kernel, width),
        "middle",
        [
            (full, BF16), (full, F32), (full, BF16), (full, BF16), ((1, channels), F32),
            ((rows * tiles, LANES), F32),
        ],
        (middle, key_li, gain_li, v, cotangent, query_mr, conv, shares, sums_all),
    )
    after = lax.ppermute(grad_conv, "ctx", [(k + 1, k) for k in range(ctx - 1)])
    final, = local_call(
        functools.partial(finish_kernel, modes), "finish", [(flat, BF16)], (u_seq, poles, shares)
    )
    final_all, = exchange([(final, "ctx", False)], sizes, 4, "gather_state")
    mixed, grad_query_li, residue_part, rate_part = local_call(
        functools.partial(state_kernel, modes),
        "state",
        [(full, BF16), (full, BF16), (flat, F32), (flat, F32)],
        (
            u_seq, g_seq, poles, weight, passing, final_all, shares_all, shares, pulled, consts,
            middle, cotangent, query_li,
        ),
        [pltpu.VMEM((rows * tiles, LANES), F32), pltpu.VMEM(flat, F32)],
    )
    gradient_key_medium, grad_norm, gain_mr_part, inner, filter_part = local_call(
        functools.partial(back_kernel, members, width),
        "back",
        [(full, BF16), (full, F32), ((1, channels), F32), ((8, rows), F32), ((groups, taps), F32)],
        (grad_conv, after, mixed_in, before, wide, tokens, key_mr, gain_mr, power_all),
    )
    parts = jnp.concatenate(
        [
            residue_part, rate_part, filter_part,
            gain_mr_part.reshape(tiles, LANES), gain_li_part.reshape(tiles, LANES),
        ],
        axis=0,
    ).astype(BF16)
    height = parts.shape[0]
    piece = -(-height // (16 * ctx)) * 16
    parts = jnp.pad(parts, ((0, piece * ctx - height), (0, 0))).reshape(ctx, piece, LANES)
    inner_all, parts_all = exchange(
        [(inner, "tp", False), (parts, "ctx", True)], sizes, 5, "gather_last"
    )
    grad_tokens, sums_own = local_call(
        functools.partial(last_kernel, width, factor),
        "last",
        [(full, BF16), ((piece, LANES), BF16)],
        (tokens, gain_mr, grad_mid, grad_norm, power_all, inner_all, parts_all),
    )
    totals, = exchange([(sums_own, "ctx", False)], sizes, 6, "gather_totals")
    totals = totals.reshape(ctx * piece, LANES)[:height].astype(F32)
    size = modes * tiles
    return (
        mixed,
        grad_tokens,
        grad_query_mr,
        gradient_key_medium,
        grad_query_li,
        grad_key_li,
        totals[2 * size + groups : 2 * size + groups + tiles].reshape(channels),
        totals[2 * size + groups + tiles :].reshape(channels),
        totals[2 * size : 2 * size + groups],
        totals[:size].reshape(modes, channels),
        totals[size : 2 * size].reshape(modes, channels),
    )


def solution(mesh):
    return jax.shard_map(
        functools.partial(body, dict(mesh.shape)),
        mesh=mesh,
        in_specs=(
            P("ctx", "tp"),
            P("ctx", "tp"),
            P("ctx", "tp"),
            P("tp"),
            P("tp", None),
            P("ctx", "tp"),
            P("ctx", "tp"),
            P("tp"),
            P(None, "tp"),
            P("ctx"),
            P(None, "tp"),
            P("ctx", "tp"),
        ),
        out_specs=(
            P("ctx", "tp"),
            P("ctx", "tp"),
            P("ctx", "tp"),
            P("ctx", "tp"),
            P("ctx", "tp"),
            P("ctx", "tp"),
            P("tp"),
            P("tp"),
            P("tp", None),
            P(None, "tp"),
            P(None, "tp"),
        ),
        check_vma=False,
    )
```

```python
import functools
import math

import jax
import jax.numpy as jnp
from jax import lax
from jax.experimental import pallas as pl
from jax.experimental.pallas import tpu as pltpu
from jax.sharding import PartitionSpec as P

EPSILON = 1e-06
LANES = 128
F32 = jnp.float32
BF16 = jnp.bfloat16
MESH = pl.DeviceIdType.MESH


def vmem(count):
    return [pl.BlockSpec(memory_space=pltpu.VMEM)] * count


def local_call(kernel, name, outs, args, scratch=(), flops=10_000_000):
    return pl.pallas_call(
        kernel,
        name=name,
        out_shape=[jax.ShapeDtypeStruct(s, d) for s, d in outs],
        in_specs=vmem(len(args)),
        out_specs=vmem(len(outs)),
        scratch_shapes=list(scratch),
        cost_estimate=pl.CostEstimate(flops=flops, bytes_accessed=8_000_000, transcendentals=0),
    )(*args)


def exchange(items, sizes, cid, name):
    count = len(items)
    axes = []
    for _, axis, _ in items:
        if axis not in axes:
            axes.append(axis)
    remote = sum(sizes[axis] - 1 for _, axis, _ in items)

    def kernel(*refs):
        ins, outs = refs[:count], refs[count : 2 * count]
        send, recv, own = refs[2 * count :]
        barrier = pltpu.get_barrier_semaphore()
        greeted = 0
        for axis in axes:
            me = lax.axis_index(axis)
            for step in range(1, sizes[axis]):
                peer = lax.rem(me + step, sizes[axis])
                pl.semaphore_signal(barrier, inc=1, device_id={axis: peer}, device_id_type=MESH)
                greeted += 1
        pl.semaphore_wait(barrier, greeted)
        copies = []
        slot = 0
        for number, (_, axis, scatter) in enumerate(items):
            me = lax.axis_index(axis)
            for step in range(1, sizes[axis]):
                peer = lax.rem(me + step, sizes[axis])
                source = ins[number].at[peer] if scatter else ins[number]
                copy = pltpu.make_async_remote_copy(
                    src_ref=source,
                    dst_ref=outs[number].at[me],
                    send_sem=send.at[slot],
                    recv_sem=recv.at[slot],
                    device_id={axis: peer},
                    device_id_type=MESH,
                )
                copy.start()
                copies.append(copy)
                slot += 1
            source = ins[number].at[me] if scatter else ins[number]
            copy = pltpu.make_async_copy(source, outs[number].at[me], own.at[number])
            copy.start()
            copies.append(copy)
        for copy in copies:
            copy.wait()

    outs = []
    for array, axis, scatter in items:
        shape = array.shape if scatter else (sizes[axis],) + array.shape
        outs.append(jax.ShapeDtypeStruct(shape, array.dtype))
    return pl.pallas_call(
        kernel,
        name=name,
        out_shape=outs,
        in_specs=vmem(count),
        out_specs=vmem(count),
        scratch_shapes=[
            pltpu.SemaphoreType.DMA((remote,)),
            pltpu.SemaphoreType.DMA((remote,)),
            pltpu.SemaphoreType.DMA((count,)),
        ],
        compiler_params=pltpu.CompilerParams(collective_id=cid, has_side_effects=True),
    )(*[array for array, _, _ in items])


class Link:
    def __init__(self, sizes, send, recv):
        self.sizes, self.send, self.recv, self.used = sizes, send, recv, 0

    def greet(self, axes):
        barrier = pltpu.get_barrier_semaphore()
        greeted = 0
        for axis in axes:
            me = lax.axis_index(axis)
            for step in range(1, self.sizes[axis]):
                peer = lax.rem(me + step, self.sizes[axis])
                pl.semaphore_signal(barrier, inc=1, device_id={axis: peer}, device_id_type=MESH)
                greeted += 1
        pl.semaphore_wait(barrier, greeted)

    def copy(self, source, target, axis, peer):
        slot = self.used
        self.used += 1
        return pltpu.make_async_remote_copy(
            src_ref=source,
            dst_ref=target,
            send_sem=self.send.at[slot],
            recv_sem=self.recv.at[slot],
            device_id={axis: peer},
            device_id_type=MESH,
        )

    def shift(self, source, target, axis, step):
        size = self.sizes[axis]
        me = lax.axis_index(axis)
        copy = self.copy(source, target, axis, lax.rem(me + step + size, size))
        sends = (me + step >= 0) & (me + step < size)
        gets = (me - step >= 0) & (me - step < size)
        pl.when(sends)(copy.start)

        def sent():
            pl.when(sends)(copy.wait_send)

        def got():
            pl.when(gets)(copy.wait_recv)

        return sent, got

    def ahead(self, source, target, axis, sign):
        me = lax.axis_index(axis)
        return [
            self.shift(source, target.at[me], axis, sign * step)
            for step in range(1, self.sizes[axis])
        ]

    def everyone(self, source, target, axis, own, scatter=False):
        size = self.sizes[axis]
        me = lax.axis_index(axis)
        waits = []
        for step in range(1, size):
            peer = lax.rem(me + step, size)
            copy = self.copy(source.at[peer] if scatter else source, target.at[me], axis, peer)
            copy.start()
            waits.append((copy.wait_send, copy.wait_recv))
        copy = pltpu.make_async_copy(source.at[me] if scatter else source, target.at[me], own)
        copy.start()
        waits.append((copy.wait,))
        return waits


def settle(waits):
    for group in waits:
        for wait in group:
            wait()


def link_call(kernel, name, cid, outs, args, copies, owns, scratch=()):
    return pl.pallas_call(
        kernel,
        name=name,
        out_shape=[jax.ShapeDtypeStruct(s, d) for s, d in outs],
        in_specs=vmem(len(args)),
        out_specs=vmem(len(outs)),
        scratch_shapes=[
            *scratch,
            pltpu.SemaphoreType.DMA((copies,)),
            pltpu.SemaphoreType.DMA((copies,)),
            pltpu.SemaphoreType.DMA((owns,)),
        ],
        compiler_params=pltpu.CompilerParams(collective_id=cid, has_side_effects=True),
    )(*args)


def column(row):
    return jnp.broadcast_to(row, (LANES, LANES)).T


def row8(partial):
    total = jnp.sum(partial, axis=1, keepdims=True)
    return jnp.broadcast_to(total, partial.shape).T[:8]


def lane_tile(j):
    return pl.ds(pl.multiple_of(j * LANES, LANES), LANES)


def total_row(ref):
    out = ref[0]
    for k in range(1, ref.shape[0]):
        out = out + ref[k]
    return out[:1]


def begin_kernel(modes, x_ref, cot_ref, q_ref, keep_ref, p_ref, w_ref, pow_ref, r_ref, g_ref, lead_ref):
    rows, channels = x_ref.shape
    tiles = channels // LANES
    lanes = lax.broadcasted_iota(jnp.int32, (8, LANES), 1)
    run = keep_ref[...]
    step = 1
    while step < LANES:
        run = run * jnp.where(lanes >= step, pltpu.roll(run, step, 1), 1.0)
        step *= 2
    r_ref[...] = run
    r_col = column(run[:1])
    total = jnp.zeros((rows, LANES), F32)
    for j in range(tiles):
        at = slice(j * LANES, (j + 1) * LANES)
        x = x_ref[:, at].astype(F32)
        total = total + x * x
        g_ref[pl.ds(j, rows, stride=tiles), :] = (
            cot_ref[:, at].astype(F32) * q_ref[:, at].astype(F32) * r_col
        )
    pow_ref[...] = row8(total)
    sub = min(8, tiles)
    for b in range(tiles // sub):
        where = [pl.ds(n * tiles + b * sub, sub) for n in range(modes)]
        pole = [p_ref[at, :] for at in where]

        def back(i, units, b=b, pole=pole):
            t = rows - 1 - i
            g = g_ref[pl.ds(pl.multiple_of(t * tiles + b * sub, sub), sub), :]
            return tuple(pole[n] * units[n] + g for n in range(modes))

        units = lax.fori_loop(
            0, rows, back, tuple(jnp.zeros((sub, LANES), F32) for _ in range(modes)), unroll=4
        )
        for n in range(modes):
            lead_ref[where[n], :] = (w_ref[where[n], :] * pole[n] * units[n]).astype(BF16)


def carried(part_ref, r_all_ref, pass_ref, ahead, reverse):
    count = part_ref.shape[0]
    order = range(count - 1, 0, -1) if reverse else range(count - 1)
    acc = jnp.zeros(pass_ref.shape, F32)
    for m in order:
        share = jnp.broadcast_to(r_all_ref[m][:1, LANES - 1 :], (1, LANES))
        new = part_ref[m].astype(F32) + pass_ref[...] * share * acc
        live = m > ahead if reverse else m < ahead
        acc = jnp.where(live, new, acc)
    return acc


def adjoint_kernel(
    modes, g_ref, p_ref, w_ref, pass_ref, lead_ref, r_all_ref, r_ref, mid_ref, key_ref, gain_ref,
    power_ref, v_ref, q_out_ref, sums_ref, v3_ref,
):
    rows, channels = v_ref.shape
    tiles = channels // LANES
    r_row = r_ref[:1, :]
    r_end = jnp.broadcast_to(r_row[:, LANES - 1 :], (1, LANES))
    q_out_ref[...] = carried(lead_ref, r_all_ref, pass_ref, lax.axis_index("ctx"), True) * r_end
    sub = min(8, tiles)
    for b in range(tiles // sub):
        where = [pl.ds(n * tiles + b * sub, sub) for n in range(modes)]
        pole = [p_ref[at, :] for at in where]
        weight = [w_ref[at, :] for at in where]
        last = pl.ds((rows - 1) * tiles + b * sub, sub)
        g = g_ref[last, :]
        start = [q_out_ref[where[n], :] + weight[n] * g for n in range(modes)]
        v3_ref[last, :] = functools.reduce(lambda a, c: a + c, start)

        def back(i, adj, b=b, pole=pole, weight=weight):
            at = pl.ds(pl.multiple_of((rows - 2 - i) * tiles + b * sub, sub), sub)
            g = g_ref[at, :]
            adj = tuple(pole[n] * adj[n] + weight[n] * g for n in range(modes))
            sums = list(adj)
            while len(sums) > 1:
                sums = [sums[k] + sums[k + 1] for k in range(0, len(sums), 2)]
            v3_ref[at, :] = sums[0]
            return adj

        lax.fori_loop(0, rows - 1, back, tuple(start), unroll=2)
    inverse = 1.0 / column(r_row)
    total = jnp.zeros((rows, LANES), F32)
    for j in range(tiles):
        at = slice(j * LANES, (j + 1) * LANES)
        v = v3_ref[pl.ds(j, rows, stride=tiles), :] * inverse
        v_ref[:, at] = v
        total = total + v * key_ref[:, at].astype(F32) * gain_ref[:, at] * mid_ref[:, at].astype(F32)
    sums_ref[0] = power_ref[...]
    sums_ref[1] = row8(total)


def mix_kernel(width, x_ref, key_ref, gain_ref, pow_ref, mixed_ref):
    scale = column(lax.rsqrt(total_row(pow_ref) / width + EPSILON))
    for j in range(x_ref.shape[1] // LANES):
        at = slice(j * LANES, (j + 1) * LANES)
        normed = x_ref[:, at].astype(F32) * gain_ref[:, at] * scale
        mixed_ref[:, at] = (key_ref[:, at].astype(F32) * normed).astype(BF16)


def conv_kernel(
    sizes, members, chunks, x_ref, q_ref, mixed_ref, flip_ref, lead_ref, share_ref,
    conv_ref, mid_ref, power_ref, prev_ref, lead_all_ref, share_all_ref, send, recv, own,
):
    rows, channels = x_ref.shape
    fold = LANES // members
    row_ids = lax.broadcasted_iota(jnp.int32, (rows, LANES), 0)
    col_ids = lax.broadcasted_iota(jnp.int32, (rows, LANES), 1)
    owner = col_ids // members
    link = Link(sizes, send, recv)
    link.greet(["ctx"])
    span = channels // chunks
    pieces = [slice(c * span, (c + 1) * span) for c in range(chunks)]
    halo = [
        link.shift(mixed_ref.at[:, piece], prev_ref.at[:, piece], "ctx", 1) for piece in pieces
    ]
    waits = link.ahead(lead_ref, lead_all_ref, "ctx", -1)
    waits += link.everyone(share_ref, share_all_ref, "ctx", own.at[0])

    @pl.when(lax.axis_index("ctx") == 0)
    def _():
        prev_ref[...] = jnp.zeros_like(prev_ref)

    def tile(j, power):
        at = lane_tile(j)
        both = jnp.concatenate([prev_ref[:, at], mixed_ref[:, at]], axis=0)
        taps = flip_ref[pl.ds(pl.multiple_of(j * fold, fold), fold), :]
        conv = jnp.zeros((rows, LANES), F32)
        for g in range(fold):
            table = pltpu.roll(
                jnp.broadcast_to(taps[g : g + 1], (rows, LANES)), 0, 1, stride=1, stride_axis=0
            )
            low = jnp.where(row_ids >= col_ids, table, 0.0).astype(BF16)
            high = jnp.where(row_ids < col_ids, table, 0.0).astype(BF16)
            out = jnp.dot(
                jnp.concatenate([high, low], axis=1), both, preferred_element_type=F32
            )
            conv = jnp.where(owner == g, out, conv)
        conv_ref[:, at] = conv
        mid = (x_ref[:, at].astype(F32) + q_ref[:, at].astype(F32) * conv).astype(BF16)
        mid_ref[:, at] = mid
        mid = mid.astype(F32)
        return power + mid * mid

    power = jnp.zeros((rows, LANES), F32)
    for c, (_, got) in enumerate(halo):
        got()
        power = lax.fori_loop(c * span // LANES, (c + 1) * span // LANES, tile, power)
    power_ref[...] = row8(power)
    for sent, _ in halo:
        sent()
    settle(waits)


def middle_kernel(
    width, mid_ref, key_ref, gain_ref, v_ref, cot_ref, qmr_ref, conv_ref, r_ref, sums_ref,
    gkey_ref, gmid_ref, gq_ref, gconv_ref, gain_part_ref, u_ref,
):
    rows, channels = v_ref.shape
    tiles = channels // LANES
    sums = sums_ref[0]
    for k in range(1, sums_ref.shape[0]):
        sums = sums + sums_ref[k]
    scale = column(lax.rsqrt(sums[0][:1] / width + EPSILON))
    pull = scale * scale * scale * column(sums[1][:1]) / width
    inverse = 1.0 / column(r_ref[:1, :])
    for j in range(tiles):
        at = slice(j * LANES, (j + 1) * LANES)
        mid = mid_ref[:, at].astype(F32)
        key = key_ref[:, at].astype(F32)
        gain = gain_ref[:, at]
        v = v_ref[:, at]
        normed = mid * gain * scale
        gkey_ref[:, at] = (v * normed).astype(BF16)
        u_ref[pl.ds(j, rows, stride=tiles), :] = key * normed * inverse
        grad = v * key
        gain_part_ref[j : j + 1, :] = jnp.sum(grad * mid * scale, axis=0, keepdims=True)
        gmid = cot_ref[:, at].astype(F32) + gain * scale * grad - mid * pull
        gmid_ref[:, at] = gmid
        gq_ref[:, at] = (gmid * conv_ref[:, at]).astype(BF16)
        gconv_ref[:, at] = (gmid * qmr_ref[:, at].astype(F32)).astype(BF16)


def finish_kernel(modes, u_ref, p_ref, r_ref, out_ref):
    tiles = p_ref.shape[0] // modes
    rows = u_ref.shape[0] // tiles
    r_end = jnp.broadcast_to(r_ref[:1, LANES - 1 :], (1, LANES))
    sub = min(8, tiles)
    for b in range(tiles // sub):
        where = [pl.ds(n * tiles + b * sub, sub) for n in range(modes)]
        pole = [p_ref[at, :] for at in where]

        def step(t, states, b=b, pole=pole):
            u = u_ref[pl.ds(pl.multiple_of(t * tiles + b * sub, sub), sub), :]
            return tuple(pole[n] * states[n] + u for n in range(modes))

        states = lax.fori_loop(
            0, rows, step, tuple(jnp.zeros((sub, LANES), F32) for _ in range(modes)), unroll=4
        )
        for n in range(modes):
            out_ref[where[n], :] = (states[n] * r_end).astype(BF16)


def state_kernel(
    sizes, modes, u_ref, g_ref, p_ref, w_ref, pass_ref, fin_ref, r_all_ref, r_ref, q_ref, c_ref,
    mid_ref, cot_ref, qli_ref, inner_ref, small_ref, mixed_ref, gq_ref, grads_ref, inner_all_ref,
    small_all_ref, y_ref, in_ref, send, recv, own,
):
    rows, channels = mid_ref.shape
    tiles = channels // LANES
    link = Link(sizes, send, recv)
    link.greet(["tp", "ctx"])
    waits = link.everyone(inner_ref, inner_all_ref, "tp", own.at[0])
    waits += link.everyone(small_ref, small_all_ref, "ctx", own.at[1], scatter=True)
    in_ref[...] = carried(fin_ref, r_all_ref, pass_ref, lax.axis_index("ctx"), False)
    sub = min(8, tiles)
    half = min(8, modes)
    zero = jnp.zeros((sub, LANES), F32)
    for b in range(tiles // sub):
        for first in range(0, modes, half):
            where = [pl.ds((first + n) * tiles + b * sub, sub) for n in range(half)]
            pole = [p_ref[at, :] for at in where]
            weight = [w_ref[at, :] for at in where]

            def step(t, carry, b=b, first=first, pole=pole, weight=weight):
                at = pl.ds(pl.multiple_of(t * tiles + b * sub, sub), sub)
                u = u_ref[at, :]
                g = g_ref[at, :]
                states, slopes, wsum, psum = carry
                slopes = tuple(pole[n] * slopes[n] + states[n] for n in range(half))
                states = tuple(pole[n] * states[n] + u for n in range(half))
                wsum = tuple(wsum[n] + g * states[n] for n in range(half))
                psum = tuple(psum[n] + g * slopes[n] for n in range(half))
                sums = [weight[n] * states[n] for n in range(half)]
                while len(sums) > 1:
                    sums = [sums[k] + sums[k + 1] for k in range(0, len(sums), 2)]
                if first == 0:
                    y_ref[at, :] = sums[0]
                else:
                    y_ref[at, :] = y_ref[at, :] + sums[0]
                return (states, slopes, wsum, psum)

            begin = tuple(in_ref[at, :] for at in where)
            zeros = (zero,) * half
            _, slopes, wsum, psum = lax.fori_loop(
                0, rows, step, (begin, zeros, zeros, zeros), unroll=2
            )
            for n in range(half):
                at = where[n]
                pgrad = weight[n] * psum[n] + q_ref[at, :] * slopes[n]
                grads_ref[0, at, :] = (c_ref[0, at, :] * wsum[n]).astype(BF16)
                grads_ref[1, at, :] = (
                    c_ref[1, at, :] * wsum[n] - c_ref[2, at, :] * pgrad
                ).astype(BF16)
    r_col = column(r_ref[:1, :])
    for j in range(tiles):
        at = slice(j * LANES, (j + 1) * LANES)
        conv = y_ref[pl.ds(j, rows, stride=tiles), :] * r_col
        mixed_ref[:, at] = (
            mid_ref[:, at].astype(F32) + qli_ref[:, at].astype(F32) * conv
        ).astype(BF16)
        gq_ref[:, at] = (cot_ref[:, at].astype(F32) * conv).astype(BF16)
    settle(waits)


def back_kernel(
    sizes, members, width, chunks, gconv_ref, mixed_ref, prev_ref, filt_ref, x_ref, key_ref,
    gain_ref, pow_ref, fin_ref, gkey_ref, gnorm_ref, gain_part_ref, inner_ref, fgrad_ref,
    fin_all_ref, next_ref, send, recv, own,
):
    rows, channels = x_ref.shape
    fold = LANES // members
    row_ids = lax.broadcasted_iota(jnp.int32, (rows, LANES), 0)
    col_ids = lax.broadcasted_iota(jnp.int32, (rows, LANES), 1)
    owner = col_ids // members
    flip = jnp.where(row_ids + col_ids == rows - 1, 1.0, 0.0).astype(BF16)
    link = Link(sizes, send, recv)
    link.greet(["ctx"])
    span = channels // chunks
    pieces = [slice(c * span, (c + 1) * span) for c in range(chunks)]
    halo = [
        link.shift(gconv_ref.at[:, piece], next_ref.at[:, piece], "ctx", -1) for piece in pieces
    ]
    waits = link.ahead(fin_ref, fin_all_ref, "ctx", 1)

    @pl.when(lax.axis_index("ctx") == sizes["ctx"] - 1)
    def _():
        next_ref[...] = jnp.zeros_like(next_ref)

    scale = column(lax.rsqrt(total_row(pow_ref) / width + EPSILON))

    def tile(j, inner):
        at = lane_tile(j)
        prev = prev_ref[:, at]
        here = gconv_ref[:, at]
        both = jnp.concatenate([here, next_ref[:, at]], axis=0)
        turned = jnp.concatenate(
            [
                jnp.dot(flip, mixed_ref[:, at], preferred_element_type=F32).astype(BF16),
                jnp.dot(flip, prev, preferred_element_type=F32).astype(BF16),
            ],
            axis=0,
        )
        rows_at = pl.ds(pl.multiple_of(j * fold, fold), fold)
        taps = filt_ref[rows_at, :]
        gmix = jnp.zeros((rows, LANES), F32)
        grads = []
        for g in range(fold):
            table = pltpu.roll(
                jnp.broadcast_to(taps[g : g + 1], (rows, LANES)), 0, 1, stride=1, stride_axis=0
            )
            low = jnp.where(col_ids >= row_ids, table, 0.0).astype(BF16)
            high = jnp.where(col_ids < row_ids, table, 0.0).astype(BF16)
            out = jnp.dot(jnp.concatenate([low, high], axis=1), both, preferred_element_type=F32)
            gmix = jnp.where(owner == g, out, gmix)
            mine = jnp.where(owner == g, here, jnp.zeros_like(here))
            pair = lax.dot_general(
                turned, mine, (((1,), (1,)), ((), ())), preferred_element_type=F32
            )
            pair = jnp.where(col_ids >= rows - 1 - row_ids, pair[:rows], pair[rows:])
            pair = pltpu.roll(pair, 1, 1, stride=1, stride_axis=0)
            grads.append(jnp.sum(pair, axis=0, keepdims=True))
        fgrad_ref[rows_at, :] = jnp.concatenate(grads, axis=0)
        x = x_ref[:, at].astype(F32)
        gain = gain_ref[:, at]
        gkey_ref[:, at] = (gmix * (x * gain * scale)).astype(BF16)
        gnorm = gmix * key_ref[:, at].astype(F32)
        gnorm_ref[:, at] = gnorm
        gain_part_ref[pl.ds(j, 1), :] = jnp.sum(gnorm * x * scale, axis=0, keepdims=True)
        return inner + gnorm * gain * x

    inner = jnp.zeros((rows, LANES), F32)
    for c, (_, got) in enumerate(halo):
        got()
        inner = lax.fori_loop(c * span // LANES, (c + 1) * span // LANES, tile, inner)
    inner_ref[...] = row8(inner)
    for sent, _ in halo:
        sent()
    settle(waits)


def last_kernel(
    sizes, width, factor, x_ref, gain_ref, gmid_ref, gnorm_ref, pow_ref, inner_ref, small_ref,
    large_ref, out_ref, small_sum_ref, large_sum_ref, large_all_ref, send, recv, own,
):
    link = Link(sizes, send, recv)
    link.greet(["ctx"])
    waits = link.everyone(large_ref, large_all_ref, "ctx", own.at[0], scatter=True)
    scale = column(lax.rsqrt(total_row(pow_ref) / width + EPSILON))
    pull = scale * scale * scale * column(total_row(inner_ref)) / width
    for j in range(x_ref.shape[1] // LANES):
        at = slice(j * LANES, (j + 1) * LANES)
        out_ref[:, at] = (
            gmid_ref[:, at]
            + gain_ref[:, at] * scale * gnorm_ref[:, at]
            - x_ref[:, at].astype(F32) * pull
        ).astype(BF16)
    settle(waits)
    for parts_ref, sum_ref in ((small_ref, small_sum_ref), (large_all_ref, large_sum_ref)):
        total = parts_ref[0].astype(F32)
        for k in range(1, parts_ref.shape[0]):
            total = total + parts_ref[k].astype(F32)
        sum_ref[...] = (total * factor).astype(BF16)


def pieces_of(parts, count):
    height = parts.shape[0]
    piece = -(-height // (16 * count)) * 16
    if piece * count > height:
        parts = jnp.pad(parts, ((0, piece * count - height), (0, 0)))
    return parts.reshape(count, piece, LANES)


def body(
    sizes,
    tokens,
    query_mr,
    key_mr,
    gain_mr,
    filter_mr,
    query_li,
    key_li,
    gain_li,
    log_rates,
    retain,
    residues,
    cotangent,
):
    rows, channels = tokens.shape
    groups, taps = filter_mr.shape
    members = channels // groups
    modes = log_rates.shape[0]
    tiles = channels // LANES
    ctx, tp = sizes["ctx"], sizes["tp"]
    width = channels * tp
    factor = 1.0 / math.sqrt(rows * ctx)
    flat = (modes * tiles, LANES)
    full = (rows, channels)

    rates = jnp.exp(log_rates.reshape(flat))
    resid = residues.reshape(flat)
    poles = jnp.exp(-rates)
    spread = jnp.sqrt(-jnp.expm1(-2.0 * rates))
    weight = resid * spread
    passing = jnp.exp(-rows * rates)
    consts = jnp.stack([spread, rates * resid * jnp.exp(-2.0 * rates) / spread, rates * poles])
    keep = jnp.broadcast_to(retain[None, :], (8, rows))
    wide = filter_mr.astype(F32)
    flipped = jnp.concatenate([wide[:, :1], wide[:, :0:-1]], axis=1)
    gain_mr = gain_mr[None, :]
    gain_li = gain_li[None, :]

    power, shares, g_seq, lead = local_call(
        functools.partial(begin_kernel, modes),
        "begin",
        [((8, rows), F32), ((8, rows), F32), ((rows * tiles, LANES), F32), (flat, BF16)],
        (tokens, cotangent, query_li, keep, poles, weight),
    )
    power_all, = exchange([(power, "tp", False)], sizes, 1, "gather_power")
    mixed_in, = local_call(
        functools.partial(mix_kernel, width), "mix", [(full, BF16)],
        (tokens, key_mr, gain_mr, power_all),
    )
    chunks = min(4, tiles)
    hops = chunks + ctx - 1
    gathered = ((ctx,) + flat, BF16)
    conv, middle, power_mid, before, lead_all, shares_all = link_call(
        functools.partial(conv_kernel, sizes, members, chunks),
        "conv",
        2,
        [
            (full, F32), (full, BF16), ((8, rows), F32), (full, BF16), gathered,
            ((ctx, 8, rows), F32),
        ],
        (tokens, query_mr, mixed_in, flipped, lead, shares),
        hops + ctx - 1,
        1,
    )
    v, pulled, sums = local_call(
        functools.partial(adjoint_kernel, modes),
        "adjoint",
        [(full, F32), (flat, F32), ((2, 8, rows), F32)],
        (
            g_seq, poles, weight, passing, lead_all, shares_all, shares, middle, key_li, gain_li,
            power_mid,
        ),
        [pltpu.VMEM((rows * tiles, LANES), F32)],
    )
    sums_all, = exchange([(sums, "tp", False)], sizes, 3, "gather_middle")
    grad_key_li, grad_mid, grad_query_mr, grad_conv, gain_li_part, u_seq = local_call(
        functools.partial(middle_kernel, width),
        "middle",
        [
            (full, BF16), (full, F32), (full, BF16), (full, BF16), ((tiles, LANES), F32),
            ((rows * tiles, LANES), F32),
        ],
        (middle, key_li, gain_li, v, cotangent, query_mr, conv, shares, sums_all),
    )
    final, = local_call(
        functools.partial(finish_kernel, modes), "finish", [(flat, BF16)], (u_seq, poles, shares)
    )
    gradient_key_medium, grad_norm, gain_mr_part, inner, filter_part, final_all, _ = link_call(
        functools.partial(back_kernel, sizes, members, width, chunks),
        "back",
        4,
        [
            (full, BF16), (full, F32), ((tiles, LANES), F32), ((8, rows), F32),
            ((groups, taps), F32), gathered, (full, BF16),
        ],
        (
            grad_conv, mixed_in, before, wide, tokens, key_mr, gain_mr, power_all, final,
        ),
        hops,
        1,
    )
    small = pieces_of(
        jnp.concatenate([filter_part, gain_mr_part, gain_li_part], axis=0).astype(BF16), ctx
    )
    mixed, grad_query_li, mode_grads, inner_all, small_all = link_call(
        functools.partial(state_kernel, sizes, modes),
        "state",
        5,
        [
            (full, BF16), (full, BF16), ((2,) + flat, BF16), ((tp, 8, rows), F32),
            (small.shape, BF16),
        ],
        (
            u_seq, g_seq, poles, weight, passing, final_all, shares_all, shares, pulled, consts,
            middle, cotangent, query_li, inner, small,
        ),
        ctx + tp - 2,
        2,
        [pltpu.VMEM((rows * tiles, LANES), F32), pltpu.VMEM(flat, F32)],
    )
    size = modes * tiles
    large = pieces_of(mode_grads.reshape(2 * size, LANES), ctx)
    grad_tokens, small_sum, large_sum, _ = link_call(
        functools.partial(last_kernel, sizes, width, factor),
        "last",
        6,
        [(full, BF16), (small.shape[1:], BF16), (large.shape[1:], BF16), (large.shape, BF16)],
        (
            tokens, gain_mr, grad_mid, grad_norm, power_all, inner_all, small_all, large,
        ),
        ctx - 1,
        1,
    )
    small_total, large_total = exchange(
        [(small_sum, "ctx", False), (large_sum, "ctx", False)], sizes, 7, "gather_totals"
    )
    small_total = small_total.reshape(-1, LANES).astype(F32)
    large_total = large_total.reshape(-1, LANES).astype(F32)
    return (
        mixed,
        grad_tokens,
        grad_query_mr,
        gradient_key_medium,
        grad_query_li,
        grad_key_li,
        small_total[groups : groups + tiles].reshape(channels),
        small_total[groups + tiles : groups + 2 * tiles].reshape(channels),
        small_total[:groups],
        large_total[:size].reshape(modes, channels),
        large_total[size : 2 * size].reshape(modes, channels),
    )


def solution(mesh):
    return jax.shard_map(
        functools.partial(body, dict(mesh.shape)),
        mesh=mesh,
        in_specs=(
            P("ctx", "tp"),
            P("ctx", "tp"),
            P("ctx", "tp"),
            P("tp"),
            P("tp", None),
            P("ctx", "tp"),
            P("ctx", "tp"),
            P("tp"),
            P(None, "tp"),
            P("ctx"),
            P(None, "tp"),
            P("ctx", "tp"),
        ),
        out_specs=(
            P("ctx", "tp"),
            P("ctx", "tp"),
            P("ctx", "tp"),
            P("ctx", "tp"),
            P("ctx", "tp"),
            P("ctx", "tp"),
            P("tp"),
            P("tp"),
            P("tp", None),
            P(None, "tp"),
            P(None, "tp"),
        ),
        check_vma=False,
    )
```

```python
import functools
import math

import jax
import jax.numpy as jnp
from jax import lax
from jax.experimental import pallas as pl
from jax.experimental.pallas import tpu as pltpu
from jax.sharding import PartitionSpec as P

EPSILON = 1e-06
LANES = 128
F32 = jnp.float32
BF16 = jnp.bfloat16
MESH = pl.DeviceIdType.MESH


def vmem(count):
    return [pl.BlockSpec(memory_space=pltpu.VMEM)] * count


def local_call(kernel, name, outs, args, scratch=(), flops=10_000_000):
    return pl.pallas_call(
        kernel,
        name=name,
        out_shape=[jax.ShapeDtypeStruct(s, d) for s, d in outs],
        in_specs=vmem(len(args)),
        out_specs=vmem(len(outs)),
        scratch_shapes=list(scratch),
        cost_estimate=pl.CostEstimate(flops=flops, bytes_accessed=8_000_000, transcendentals=0),
    )(*args)


def exchange(items, sizes, cid, name):
    count = len(items)
    axes = []
    for _, axis, _ in items:
        if axis not in axes:
            axes.append(axis)
    remote = sum(sizes[axis] - 1 for _, axis, _ in items)

    def kernel(*refs):
        ins, outs = refs[:count], refs[count : 2 * count]
        send, recv, own = refs[2 * count :]
        barrier = pltpu.get_barrier_semaphore()
        greeted = 0
        for axis in axes:
            me = lax.axis_index(axis)
            for step in range(1, sizes[axis]):
                peer = lax.rem(me + step, sizes[axis])
                pl.semaphore_signal(barrier, inc=1, device_id={axis: peer}, device_id_type=MESH)
                greeted += 1
        pl.semaphore_wait(barrier, greeted)
        copies = []
        slot = 0
        for number, (_, axis, scatter) in enumerate(items):
            me = lax.axis_index(axis)
            for step in range(1, sizes[axis]):
                peer = lax.rem(me + step, sizes[axis])
                source = ins[number].at[peer] if scatter else ins[number]
                copy = pltpu.make_async_remote_copy(
                    src_ref=source,
                    dst_ref=outs[number].at[me],
                    send_sem=send.at[slot],
                    recv_sem=recv.at[slot],
                    device_id={axis: peer},
                    device_id_type=MESH,
                )
                copy.start()
                copies.append(copy)
                slot += 1
            source = ins[number].at[me] if scatter else ins[number]
            copy = pltpu.make_async_copy(source, outs[number].at[me], own.at[number])
            copy.start()
            copies.append(copy)
        for copy in copies:
            copy.wait()

    outs = []
    for array, axis, scatter in items:
        shape = array.shape if scatter else (sizes[axis],) + array.shape
        outs.append(jax.ShapeDtypeStruct(shape, array.dtype))
    return pl.pallas_call(
        kernel,
        name=name,
        out_shape=outs,
        in_specs=vmem(count),
        out_specs=vmem(count),
        scratch_shapes=[
            pltpu.SemaphoreType.DMA((remote,)),
            pltpu.SemaphoreType.DMA((remote,)),
            pltpu.SemaphoreType.DMA((count,)),
        ],
        compiler_params=pltpu.CompilerParams(collective_id=cid, has_side_effects=True),
    )(*[array for array, _, _ in items])


class Link:
    def __init__(self, sizes, send, recv):
        self.sizes, self.send, self.recv, self.used = sizes, send, recv, 0

    def greet(self, axes):
        barrier = pltpu.get_barrier_semaphore()
        greeted = 0
        for axis in axes:
            me = lax.axis_index(axis)
            for step in range(1, self.sizes[axis]):
                peer = lax.rem(me + step, self.sizes[axis])
                pl.semaphore_signal(barrier, inc=1, device_id={axis: peer}, device_id_type=MESH)
                greeted += 1
        pl.semaphore_wait(barrier, greeted)

    def copy(self, source, target, axis, peer):
        slot = self.used
        self.used += 1
        return pltpu.make_async_remote_copy(
            src_ref=source,
            dst_ref=target,
            send_sem=self.send.at[slot],
            recv_sem=self.recv.at[slot],
            device_id={axis: peer},
            device_id_type=MESH,
        )

    def shift(self, source, target, axis, step):
        size = self.sizes[axis]
        me = lax.axis_index(axis)
        copy = self.copy(source, target, axis, lax.rem(me + step + size, size))
        sends = (me + step >= 0) & (me + step < size)
        gets = (me - step >= 0) & (me - step < size)
        pl.when(sends)(copy.start)

        def sent():
            pl.when(sends)(copy.wait_send)

        def got():
            pl.when(gets)(copy.wait_recv)

        return sent, got

    def everyone(self, source, target, axis, own, scatter=False):
        size = self.sizes[axis]
        me = lax.axis_index(axis)
        waits = []
        for step in range(1, size):
            peer = lax.rem(me + step, size)
            copy = self.copy(source.at[peer] if scatter else source, target.at[me], axis, peer)
            copy.start()
            waits.append((copy.wait_send, copy.wait_recv))
        copy = pltpu.make_async_copy(source.at[me] if scatter else source, target.at[me], own)
        copy.start()
        waits.append((copy.wait,))
        return waits


def settle(waits):
    for group in waits:
        for wait in group:
            wait()


def link_call(kernel, name, cid, outs, args, copies, owns, scratch=()):
    return pl.pallas_call(
        kernel,
        name=name,
        out_shape=[jax.ShapeDtypeStruct(s, d) for s, d in outs],
        in_specs=vmem(len(args)),
        out_specs=vmem(len(outs)),
        scratch_shapes=[
            *scratch,
            pltpu.SemaphoreType.DMA((copies,)),
            pltpu.SemaphoreType.DMA((copies,)),
            pltpu.SemaphoreType.DMA((owns,)),
        ],
        compiler_params=pltpu.CompilerParams(collective_id=cid, has_side_effects=True),
    )(*args)


def column(row):
    return jnp.broadcast_to(row, (LANES, LANES)).T


def row8(partial):
    total = jnp.sum(partial, axis=1, keepdims=True)
    return jnp.broadcast_to(total, partial.shape).T[:8]


def lane_tile(j):
    return pl.ds(pl.multiple_of(j * LANES, LANES), LANES)


def total_row(ref):
    out = ref[0]
    for k in range(1, ref.shape[0]):
        out = out + ref[k]
    return out[:1]


def begin_kernel(modes, x_ref, cot_ref, q_ref, keep_ref, p_ref, w_ref, pow_ref, r_ref, g_ref, lead_ref):
    rows, channels = x_ref.shape
    tiles = channels // LANES
    lanes = lax.broadcasted_iota(jnp.int32, (8, LANES), 1)
    run = keep_ref[...]
    step = 1
    while step < LANES:
        run = run * jnp.where(lanes >= step, pltpu.roll(run, step, 1), 1.0)
        step *= 2
    r_ref[...] = run
    r_col = column(run[:1])
    total = jnp.zeros((rows, LANES), F32)
    for j in range(tiles):
        at = slice(j * LANES, (j + 1) * LANES)
        x = x_ref[:, at].astype(F32)
        total = total + x * x
        g_ref[pl.ds(j, rows, stride=tiles), :] = (
            cot_ref[:, at].astype(F32) * q_ref[:, at].astype(F32) * r_col
        )
    pow_ref[...] = row8(total)
    sub = min(8, tiles)
    for b in range(tiles // sub):
        where = [pl.ds(n * tiles + b * sub, sub) for n in range(modes)]
        pole = [p_ref[at, :] for at in where]

        def back(i, units, b=b, pole=pole):
            t = rows - 1 - i
            g = g_ref[pl.ds(pl.multiple_of(t * tiles + b * sub, sub), sub), :]
            return tuple(pole[n] * units[n] + g for n in range(modes))

        units = lax.fori_loop(
            0, rows, back, tuple(jnp.zeros((sub, LANES), F32) for _ in range(modes)), unroll=4
        )
        for n in range(modes):
            lead_ref[where[n], :] = (w_ref[where[n], :] * pole[n] * units[n]).astype(BF16)


def doubling(link, own_ref, got_ref, part_ref, share_all_ref, pass_ref, out_ref, sign, ready):
    size = link.sizes["ctx"]
    me = lax.axis_index("ctx")
    rounds = got_ref.shape[0]
    sends = [None] * rounds
    sends[0] = link.shift(own_ref, got_ref.at[0], "ctx", sign)

    def share(index):
        row = share_all_ref[lax.rem(index + size, size)][:1, LANES - 1 :]
        return jnp.broadcast_to(row, (1, LANES))

    def receive(k):
        if k == 0:
            ready()
        sends[k][1]()
        reach = 2**k
        source = me - sign * reach
        live = (source >= 0) & (source < size)
        value = jnp.where(live, got_ref[k].astype(F32), 0.0)
        if k > 0:
            factor = pass_ref[...]
            for step in range(1, k):
                factor = factor * factor * pass_ref[...]
            scale = share(me - sign)
            for step in range(2, reach):
                scale = scale * share(me - sign * step)
            value = out_ref[...] + factor * scale * value
        out_ref[...] = value
        if k < rounds - 1:
            joined = own_ref[...].astype(F32) + pass_ref[...] * share(me) * value
            part_ref[k] = joined.astype(BF16)

    def send(k):
        sends[k] = link.shift(part_ref.at[k - 1], got_ref.at[k], "ctx", sign * 2**k)

    stages = [functools.partial(receive, 0)]
    for k in range(1, rounds):
        stages += [functools.partial(send, k), functools.partial(receive, k)]

    def done():
        for sent, _ in sends:
            sent()

    return stages, done


def adjoint_kernel(
    modes, g_ref, p_ref, w_ref, lead_ref, r_ref, mid_ref, key_ref, gain_ref,
    power_ref, v_ref, q_out_ref, sums_ref, v3_ref,
):
    rows, channels = v_ref.shape
    tiles = channels // LANES
    r_row = r_ref[:1, :]
    r_end = jnp.broadcast_to(r_row[:, LANES - 1 :], (1, LANES))
    q_out_ref[...] = lead_ref[...] * r_end
    sub = min(8, tiles)
    for b in range(tiles // sub):
        where = [pl.ds(n * tiles + b * sub, sub) for n in range(modes)]
        pole = [p_ref[at, :] for at in where]
        weight = [w_ref[at, :] for at in where]
        last = pl.ds((rows - 1) * tiles + b * sub, sub)
        g = g_ref[last, :]
        start = [q_out_ref[where[n], :] + weight[n] * g for n in range(modes)]
        v3_ref[last, :] = functools.reduce(lambda a, c: a + c, start)

        def back(i, adj, b=b, pole=pole, weight=weight):
            at = pl.ds(pl.multiple_of((rows - 2 - i) * tiles + b * sub, sub), sub)
            g = g_ref[at, :]
            adj = tuple(pole[n] * adj[n] + weight[n] * g for n in range(modes))
            sums = list(adj)
            while len(sums) > 1:
                sums = [sums[k] + sums[k + 1] for k in range(0, len(sums), 2)]
            v3_ref[at, :] = sums[0]
            return adj

        lax.fori_loop(0, rows - 1, back, tuple(start), unroll=2)
    inverse = 1.0 / column(r_row)
    total = jnp.zeros((rows, LANES), F32)
    for j in range(tiles):
        at = slice(j * LANES, (j + 1) * LANES)
        v = v3_ref[pl.ds(j, rows, stride=tiles), :] * inverse
        v_ref[:, at] = v
        total = total + v * key_ref[:, at].astype(F32) * gain_ref[:, at] * mid_ref[:, at].astype(F32)
    sums_ref[0] = power_ref[...]
    sums_ref[1] = row8(total)


def mix_kernel(width, x_ref, key_ref, gain_ref, pow_ref, mixed_ref):
    scale = column(lax.rsqrt(total_row(pow_ref) / width + EPSILON))
    for j in range(x_ref.shape[1] // LANES):
        at = slice(j * LANES, (j + 1) * LANES)
        normed = x_ref[:, at].astype(F32) * gain_ref[:, at] * scale
        mixed_ref[:, at] = (key_ref[:, at].astype(F32) * normed).astype(BF16)


def conv_kernel(
    sizes, members, chunks, x_ref, q_ref, mixed_ref, flip_ref, lead_ref, share_ref, pass_ref,
    conv_ref, mid_ref, power_ref, prev_ref, lead_all_ref, share_all_ref, got_ref, part_ref,
    send, recv, own,
):
    rows, channels = x_ref.shape
    fold = LANES // members
    row_ids = lax.broadcasted_iota(jnp.int32, (rows, LANES), 0)
    col_ids = lax.broadcasted_iota(jnp.int32, (rows, LANES), 1)
    owner = col_ids // members
    link = Link(sizes, send, recv)
    link.greet(["ctx"])
    span = channels // chunks
    pieces = [slice(c * span, (c + 1) * span) for c in range(chunks)]
    waits = link.everyone(share_ref, share_all_ref, "ctx", own.at[0])
    stages, done = doubling(
        link, lead_ref, got_ref, part_ref, share_all_ref, pass_ref, lead_all_ref, -1,
        lambda: settle(waits),
    )
    halo = [
        link.shift(mixed_ref.at[:, piece], prev_ref.at[:, piece], "ctx", 1) for piece in pieces
    ]

    @pl.when(lax.axis_index("ctx") == 0)
    def _():
        prev_ref[...] = jnp.zeros_like(prev_ref)

    def tile(j, power):
        at = lane_tile(j)
        both = jnp.concatenate([prev_ref[:, at], mixed_ref[:, at]], axis=0)
        taps = flip_ref[pl.ds(pl.multiple_of(j * fold, fold), fold), :]
        conv = jnp.zeros((rows, LANES), F32)
        for g in range(fold):
            table = pltpu.roll(
                jnp.broadcast_to(taps[g : g + 1], (rows, LANES)), 0, 1, stride=1, stride_axis=0
            )
            low = jnp.where(row_ids >= col_ids, table, 0.0).astype(BF16)
            high = jnp.where(row_ids < col_ids, table, 0.0).astype(BF16)
            out = jnp.dot(
                jnp.concatenate([high, low], axis=1), both, preferred_element_type=F32
            )
            conv = jnp.where(owner == g, out, conv)
        conv_ref[:, at] = conv
        mid = (x_ref[:, at].astype(F32) + q_ref[:, at].astype(F32) * conv).astype(BF16)
        mid_ref[:, at] = mid
        mid = mid.astype(F32)
        return power + mid * mid

    power = jnp.zeros((rows, LANES), F32)
    for c, (_, got) in enumerate(halo):
        if c < len(stages):
            stages[c]()
        got()
        power = lax.fori_loop(c * span // LANES, (c + 1) * span // LANES, tile, power)
    power_ref[...] = row8(power)
    for stage in stages[chunks:]:
        stage()
    for sent, _ in halo:
        sent()
    done()


def middle_kernel(
    width, mid_ref, key_ref, gain_ref, v_ref, cot_ref, qmr_ref, conv_ref, r_ref, sums_ref,
    gkey_ref, gmid_ref, gq_ref, gconv_ref, gain_part_ref, u_ref,
):
    rows, channels = v_ref.shape
    tiles = channels // LANES
    sums = sums_ref[0]
    for k in range(1, sums_ref.shape[0]):
        sums = sums + sums_ref[k]
    scale = column(lax.rsqrt(sums[0][:1] / width + EPSILON))
    pull = scale * scale * scale * column(sums[1][:1]) / width
    inverse = 1.0 / column(r_ref[:1, :])
    for j in range(tiles):
        at = slice(j * LANES, (j + 1) * LANES)
        mid = mid_ref[:, at].astype(F32)
        key = key_ref[:, at].astype(F32)
        gain = gain_ref[:, at]
        v = v_ref[:, at]
        normed = mid * gain * scale
        gkey_ref[:, at] = (v * normed).astype(BF16)
        u_ref[pl.ds(j, rows, stride=tiles), :] = key * normed * inverse
        grad = v * key
        gain_part_ref[j : j + 1, :] = jnp.sum(grad * mid * scale, axis=0, keepdims=True)
        gmid = cot_ref[:, at].astype(F32) + gain * scale * grad - mid * pull
        gmid_ref[:, at] = gmid
        gq_ref[:, at] = (gmid * conv_ref[:, at]).astype(BF16)
        gconv_ref[:, at] = (gmid * qmr_ref[:, at].astype(F32)).astype(BF16)


def finish_kernel(modes, u_ref, p_ref, r_ref, out_ref):
    tiles = p_ref.shape[0] // modes
    rows = u_ref.shape[0] // tiles
    r_end = jnp.broadcast_to(r_ref[:1, LANES - 1 :], (1, LANES))
    sub = min(8, tiles)
    for b in range(tiles // sub):
        where = [pl.ds(n * tiles + b * sub, sub) for n in range(modes)]
        pole = [p_ref[at, :] for at in where]

        def step(t, states, b=b, pole=pole):
            u = u_ref[pl.ds(pl.multiple_of(t * tiles + b * sub, sub), sub), :]
            return tuple(pole[n] * states[n] + u for n in range(modes))

        states = lax.fori_loop(
            0, rows, step, tuple(jnp.zeros((sub, LANES), F32) for _ in range(modes)), unroll=4
        )
        for n in range(modes):
            out_ref[where[n], :] = (states[n] * r_end).astype(BF16)


def state_kernel(
    sizes, modes, u_ref, g_ref, p_ref, w_ref, in_ref, r_ref, q_ref, c_ref,
    mid_ref, cot_ref, qli_ref, inner_ref, small_ref, mixed_ref, gq_ref, grads_ref, inner_all_ref,
    small_all_ref, y_ref, send, recv, own,
):
    rows, channels = mid_ref.shape
    tiles = channels // LANES
    link = Link(sizes, send, recv)
    link.greet(["tp", "ctx"])
    waits = link.everyone(inner_ref, inner_all_ref, "tp", own.at[0])
    waits += link.everyone(small_ref, small_all_ref, "ctx", own.at[1], scatter=True)
    sub = min(8, tiles)
    half = min(8, modes)
    zero = jnp.zeros((sub, LANES), F32)
    for b in range(tiles // sub):
        for first in range(0, modes, half):
            where = [pl.ds((first + n) * tiles + b * sub, sub) for n in range(half)]
            pole = [p_ref[at, :] for at in where]
            weight = [w_ref[at, :] for at in where]

            def step(t, carry, b=b, first=first, pole=pole, weight=weight):
                at = pl.ds(pl.multiple_of(t * tiles + b * sub, sub), sub)
                u = u_ref[at, :]
                g = g_ref[at, :]
                states, slopes, wsum, psum = carry
                slopes = tuple(pole[n] * slopes[n] + states[n] for n in range(half))
                states = tuple(pole[n] * states[n] + u for n in range(half))
                wsum = tuple(wsum[n] + g * states[n] for n in range(half))
                psum = tuple(psum[n] + g * slopes[n] for n in range(half))
                sums = [weight[n] * states[n] for n in range(half)]
                while len(sums) > 1:
                    sums = [sums[k] + sums[k + 1] for k in range(0, len(sums), 2)]
                if first == 0:
                    y_ref[at, :] = sums[0]
                else:
                    y_ref[at, :] = y_ref[at, :] + sums[0]
                return (states, slopes, wsum, psum)

            begin = tuple(in_ref[at, :] for at in where)
            zeros = (zero,) * half
            _, slopes, wsum, psum = lax.fori_loop(
                0, rows, step, (begin, zeros, zeros, zeros), unroll=2
            )
            for n in range(half):
                at = where[n]
                pgrad = weight[n] * psum[n] + q_ref[at, :] * slopes[n]
                grads_ref[0, at, :] = (c_ref[0, at, :] * wsum[n]).astype(BF16)
                grads_ref[1, at, :] = (
                    c_ref[1, at, :] * wsum[n] - c_ref[2, at, :] * pgrad
                ).astype(BF16)
    r_col = column(r_ref[:1, :])
    for j in range(tiles):
        at = slice(j * LANES, (j + 1) * LANES)
        conv = y_ref[pl.ds(j, rows, stride=tiles), :] * r_col
        mixed_ref[:, at] = (
            mid_ref[:, at].astype(F32) + qli_ref[:, at].astype(F32) * conv
        ).astype(BF16)
        gq_ref[:, at] = (cot_ref[:, at].astype(F32) * conv).astype(BF16)
    settle(waits)


def back_kernel(
    sizes, members, width, chunks, gconv_ref, mixed_ref, prev_ref, filt_ref, x_ref, key_ref,
    gain_ref, pow_ref, fin_ref, share_all_ref, pass_ref, gkey_ref, gnorm_ref, gain_part_ref, inner_ref, fgrad_ref,
    fin_all_ref, next_ref, got_ref, part_ref, send, recv, own,
):
    rows, channels = x_ref.shape
    fold = LANES // members
    row_ids = lax.broadcasted_iota(jnp.int32, (rows, LANES), 0)
    col_ids = lax.broadcasted_iota(jnp.int32, (rows, LANES), 1)
    owner = col_ids // members
    flip = jnp.where(row_ids + col_ids == rows - 1, 1.0, 0.0).astype(BF16)
    link = Link(sizes, send, recv)
    link.greet(["ctx"])
    span = channels // chunks
    pieces = [slice(c * span, (c + 1) * span) for c in range(chunks)]
    stages, done = doubling(
        link, fin_ref, got_ref, part_ref, share_all_ref, pass_ref, fin_all_ref, 1, lambda: None
    )
    halo = [
        link.shift(gconv_ref.at[:, piece], next_ref.at[:, piece], "ctx", -1) for piece in pieces
    ]

    @pl.when(lax.axis_index("ctx") == sizes["ctx"] - 1)
    def _():
        next_ref[...] = jnp.zeros_like(next_ref)

    scale = column(lax.rsqrt(total_row(pow_ref) / width + EPSILON))

    def tile(j, inner):
        at = lane_tile(j)
        prev = prev_ref[:, at]
        here = gconv_ref[:, at]
        both = jnp.concatenate([here, next_ref[:, at]], axis=0)
        turned = jnp.concatenate(
            [
                jnp.dot(flip, mixed_ref[:, at], preferred_element_type=F32).astype(BF16),
                jnp.dot(flip, prev, preferred_element_type=F32).astype(BF16),
            ],
            axis=0,
        )
        rows_at = pl.ds(pl.multiple_of(j * fold, fold), fold)
        taps = filt_ref[rows_at, :]
        gmix = jnp.zeros((rows, LANES), F32)
        grads = []
        for g in range(fold):
            table = pltpu.roll(
                jnp.broadcast_to(taps[g : g + 1], (rows, LANES)), 0, 1, stride=1, stride_axis=0
            )
            low = jnp.where(col_ids >= row_ids, table, 0.0).astype(BF16)
            high = jnp.where(col_ids < row_ids, table, 0.0).astype(BF16)
            out = jnp.dot(jnp.concatenate([low, high], axis=1), both, preferred_element_type=F32)
            gmix = jnp.where(owner == g, out, gmix)
            mine = jnp.where(owner == g, here, jnp.zeros_like(here))
            pair = lax.dot_general(
                turned, mine, (((1,), (1,)), ((), ())), preferred_element_type=F32
            )
            pair = jnp.where(col_ids >= rows - 1 - row_ids, pair[:rows], pair[rows:])
            pair = pltpu.roll(pair, 1, 1, stride=1, stride_axis=0)
            grads.append(jnp.sum(pair, axis=0, keepdims=True))
        fgrad_ref[rows_at, :] = jnp.concatenate(grads, axis=0)
        x = x_ref[:, at].astype(F32)
        gain = gain_ref[:, at]
        gkey_ref[:, at] = (gmix * (x * gain * scale)).astype(BF16)
        gnorm = gmix * key_ref[:, at].astype(F32)
        gnorm_ref[:, at] = gnorm
        gain_part_ref[pl.ds(j, 1), :] = jnp.sum(gnorm * x * scale, axis=0, keepdims=True)
        return inner + gnorm * gain * x

    inner = jnp.zeros((rows, LANES), F32)
    for c, (_, got) in enumerate(halo):
        if c < len(stages):
            stages[c]()
        got()
        inner = lax.fori_loop(c * span // LANES, (c + 1) * span // LANES, tile, inner)
    inner_ref[...] = row8(inner)
    for stage in stages[chunks:]:
        stage()
    for sent, _ in halo:
        sent()
    done()


def last_kernel(
    sizes, width, factor, x_ref, gain_ref, gmid_ref, gnorm_ref, pow_ref, inner_ref, small_ref,
    large_ref, out_ref, small_sum_ref, large_sum_ref, large_all_ref, send, recv, own,
):
    link = Link(sizes, send, recv)
    link.greet(["ctx"])
    waits = link.everyone(large_ref, large_all_ref, "ctx", own.at[0], scatter=True)
    scale = column(lax.rsqrt(total_row(pow_ref) / width + EPSILON))
    pull = scale * scale * scale * column(total_row(inner_ref)) / width
    for j in range(x_ref.shape[1] // LANES):
        at = slice(j * LANES, (j + 1) * LANES)
        out_ref[:, at] = (
            gmid_ref[:, at]
            + gain_ref[:, at] * scale * gnorm_ref[:, at]
            - x_ref[:, at].astype(F32) * pull
        ).astype(BF16)
    settle(waits)
    for parts_ref, sum_ref in ((small_ref, small_sum_ref), (large_all_ref, large_sum_ref)):
        total = parts_ref[0].astype(F32)
        for k in range(1, parts_ref.shape[0]):
            total = total + parts_ref[k].astype(F32)
        sum_ref[...] = (total * factor).astype(BF16)


def pieces_of(parts, count):
    height = parts.shape[0]
    piece = -(-height // (16 * count)) * 16
    if piece * count > height:
        parts = jnp.pad(parts, ((0, piece * count - height), (0, 0)))
    return parts.reshape(count, piece, LANES)


def body(
    sizes,
    tokens,
    query_mr,
    key_mr,
    gain_mr,
    filter_mr,
    query_li,
    key_li,
    gain_li,
    log_rates,
    retain,
    residues,
    cotangent,
):
    rows, channels = tokens.shape
    groups, taps = filter_mr.shape
    members = channels // groups
    modes = log_rates.shape[0]
    tiles = channels // LANES
    ctx, tp = sizes["ctx"], sizes["tp"]
    width = channels * tp
    factor = 1.0 / math.sqrt(rows * ctx)
    flat = (modes * tiles, LANES)
    full = (rows, channels)

    rates = jnp.exp(log_rates.reshape(flat))
    resid = residues.reshape(flat)
    poles = jnp.exp(-rates)
    spread = jnp.sqrt(-jnp.expm1(-2.0 * rates))
    weight = resid * spread
    passing = jnp.exp(-rows * rates)
    consts = jnp.stack([spread, rates * resid * jnp.exp(-2.0 * rates) / spread, rates * poles])
    keep = jnp.broadcast_to(retain[None, :], (8, rows))
    wide = filter_mr.astype(F32)
    flipped = jnp.concatenate([wide[:, :1], wide[:, :0:-1]], axis=1)
    gain_mr = gain_mr[None, :]
    gain_li = gain_li[None, :]

    power, shares, g_seq, lead = local_call(
        functools.partial(begin_kernel, modes),
        "begin",
        [((8, rows), F32), ((8, rows), F32), ((rows * tiles, LANES), F32), (flat, BF16)],
        (tokens, cotangent, query_li, keep, poles, weight),
    )
    power_all, = exchange([(power, "tp", False)], sizes, 1, "gather_power")
    mixed_in, = local_call(
        functools.partial(mix_kernel, width), "mix", [(full, BF16)],
        (tokens, key_mr, gain_mr, power_all),
    )
    chunks = min(4, tiles)
    rounds = max(1, (ctx - 1).bit_length())
    hops = chunks + rounds
    gathered = (flat, F32)
    slots = [
        pltpu.VMEM((rounds,) + flat, BF16), pltpu.VMEM((max(1, rounds - 1),) + flat, BF16),
    ]
    conv, middle, power_mid, before, lead_all, shares_all = link_call(
        functools.partial(conv_kernel, sizes, members, chunks),
        "conv",
        2,
        [
            (full, F32), (full, BF16), ((8, rows), F32), (full, BF16), gathered,
            ((ctx, 8, rows), F32),
        ],
        (tokens, query_mr, mixed_in, flipped, lead, shares, passing),
        hops + ctx - 1,
        1,
        slots,
    )
    v, pulled, sums = local_call(
        functools.partial(adjoint_kernel, modes),
        "adjoint",
        [(full, F32), (flat, F32), ((2, 8, rows), F32)],
        (
            g_seq, poles, weight, lead_all, shares, middle, key_li, gain_li,
            power_mid,
        ),
        [pltpu.VMEM((rows * tiles, LANES), F32)],
    )
    sums_all, = exchange([(sums, "tp", False)], sizes, 3, "gather_middle")
    grad_key_li, grad_mid, grad_query_mr, grad_conv, gain_li_part, u_seq = local_call(
        functools.partial(middle_kernel, width),
        "middle",
        [
            (full, BF16), (full, F32), (full, BF16), (full, BF16), ((tiles, LANES), F32),
            ((rows * tiles, LANES), F32),
        ],
        (middle, key_li, gain_li, v, cotangent, query_mr, conv, shares, sums_all),
    )
    final, = local_call(
        functools.partial(finish_kernel, modes), "finish", [(flat, BF16)], (u_seq, poles, shares)
    )
    gradient_key_medium, grad_norm, gain_mr_part, inner, filter_part, final_all, _ = link_call(
        functools.partial(back_kernel, sizes, members, width, chunks),
        "back",
        4,
        [
            (full, BF16), (full, F32), ((tiles, LANES), F32), ((8, rows), F32),
            ((groups, taps), F32), gathered, (full, BF16),
        ],
        (
            grad_conv, mixed_in, before, wide, tokens, key_mr, gain_mr, power_all, final,
            shares_all, passing,
        ),
        hops,
        1,
        slots,
    )
    small = pieces_of(
        jnp.concatenate([filter_part, gain_mr_part, gain_li_part], axis=0).astype(BF16), ctx
    )
    mixed, grad_query_li, mode_grads, inner_all, small_all = link_call(
        functools.partial(state_kernel, sizes, modes),
        "state",
        5,
        [
            (full, BF16), (full, BF16), ((2,) + flat, BF16), ((tp, 8, rows), F32),
            (small.shape, BF16),
        ],
        (
            u_seq, g_seq, poles, weight, final_all, shares, pulled, consts,
            middle, cotangent, query_li, inner, small,
        ),
        ctx + tp - 2,
        2,
        [pltpu.VMEM((rows * tiles, LANES), F32)],
    )
    size = modes * tiles
    large = pieces_of(mode_grads.reshape(2 * size, LANES), ctx)
    grad_tokens, small_sum, large_sum, _ = link_call(
        functools.partial(last_kernel, sizes, width, factor),
        "last",
        6,
        [(full, BF16), (small.shape[1:], BF16), (large.shape[1:], BF16), (large.shape, BF16)],
        (
            tokens, gain_mr, grad_mid, grad_norm, power_all, inner_all, small_all, large,
        ),
        ctx - 1,
        1,
    )
    small_total, large_total = exchange(
        [(small_sum, "ctx", False), (large_sum, "ctx", False)], sizes, 7, "gather_totals"
    )
    small_total = small_total.reshape(-1, LANES).astype(F32)
    large_total = large_total.reshape(-1, LANES).astype(F32)
    return (
        mixed,
        grad_tokens,
        grad_query_mr,
        gradient_key_medium,
        grad_query_li,
        grad_key_li,
        small_total[groups : groups + tiles].reshape(channels),
        small_total[groups + tiles : groups + 2 * tiles].reshape(channels),
        small_total[:groups],
        large_total[:size].reshape(modes, channels),
        large_total[size : 2 * size].reshape(modes, channels),
    )


def solution(mesh):
    return jax.shard_map(
        functools.partial(body, dict(mesh.shape)),
        mesh=mesh,
        in_specs=(
            P("ctx", "tp"),
            P("ctx", "tp"),
            P("ctx", "tp"),
            P("tp"),
            P("tp", None),
            P("ctx", "tp"),
            P("ctx", "tp"),
            P("tp"),
            P(None, "tp"),
            P("ctx"),
            P(None, "tp"),
            P("ctx", "tp"),
        ),
        out_specs=(
            P("ctx", "tp"),
            P("ctx", "tp"),
            P("ctx", "tp"),
            P("ctx", "tp"),
            P("ctx", "tp"),
            P("ctx", "tp"),
            P("tp"),
            P("tp"),
            P("tp", None),
            P(None, "tp"),
            P(None, "tp"),
        ),
        check_vma=False,
    )
```
